32 devices in a mesh: gx: 8 (over y, x, core), gy: 4 (over z).
Axes of the slice: x: 2, y: 2, z: 4, core: 2. Of those that a mesh axis runs over, the one named last changes fastest.
Arguments:
- slip_field: float32 [256, 3, 128], P(('gy', 'gx')), may hold values from -6 to 6
- positions: float32 [256, 3, 128], P(('gy', 'gx')), may hold values from -6 to 6
- neighbours: int32 [256, 8], P(('gy', 'gx')), may hold values from 0 to 63, as said below
- near_counts: int32 [256], P(('gy', 'gx')), may hold values from 1 to 8, as said below
- cluster_basis: float32 [256, 16, 3, 128], P(('gy', 'gx')), may hold values from -0.4375 to 0.4375
- transfer: float32 [62, 16, 16], replicated, may hold values from -1 to 1
- coupling: float32 [62, 16, 16], replicated, may hold values from -1.5 to 1.5
- prestress: float32 [256, 3, 128], P(('gy', 'gx')), may hold values from -6 to 6
- normal_stress: float32 [256, 128], P(('gy', 'gx')), may hold values from 1 to 3
- friction: float32 [256, 128], P(('gy', 'gx')), may hold values from 0.3 to 0.9
- compliance: float32 [256, 128], P(('gy', 'gx')), may hold values from 0.1 to 1
- slip_state: int32 [256, 128], P(('gy', 'gx')), may hold values 0 or 1
- cell_index: int32 [256, 4, 128], P(('gy', 'gx')), may hold values from 0 to 8191, as said below
- cell_weight: float32 [256, 4, 128], P(('gy', 'gx')), may hold values from 0.1 to 0.5
- dilation: float32 [256, 128], P(('gy', 'gx')), may hold values from 1 to 10
- pressure: float32 [64, 512], P('gx', 'gy'), may hold values from -4 to 4
- mobility: float32 [64, 512], P('gx', 'gy'), may hold values from 0.05 to 0.24
Outputs:
- final_slip: float32 [256, 3, 128], P(('gy', 'gx'))
- final_pressure: float32 [64, 512], P('gx', 'gy')
The draws below stay inside these ranges and needn't reach their ends.
Inputs may be any that keep to these rules, and one draw needn't show every extreme that they name: `neighbours`: entry 0 of a row is the cluster's own number within its subtree; the entries of a row are distinct and lie within 8 clusters of the cluster's own number, counted cyclically within its subtree of 64 clusters. Only the first near_counts[c] entries of a row of neighbours are used; some cluster has exactly 8. `slip_state`: 1 marks an element that slips. `cell_index`: the four cells of an element are band rows r and r + 1 (counted cyclically over the 64 rows) at columns b and b + 1 of the band, in that order: (r, b), (r + 1, b), (r, b + 1), (r + 1, b + 1). For an element of cluster c with j = (c % 64) // 8, both rows lie in (j - 1) * 8 to (j + 2) * 8 - 1, cyclically; both ends are reached in every draw.
All inputs are finite; a program needn't handle non-finite values. No bound on the sum of `slip_state` on one device may be relied on, other than what follows from the above.
Results may differ from the reference program's by a relative error of at most 0.00027.
Values sent between devices are 32-bit elements; how exact they have to be, the bound alone decides.
A program may use at most 64 MiB of HBM per device.

```python
import math
import jax
import jax.numpy as jnp
from jax import lax

CSIZE = 128
CL_DEV = 8
NB = 8
RANK = 16
IW = 4
FX_DEV = 8
FY_DEV = 128
ITERS = 2
FLOW_STEPS = 2
NODES = 62
NC = 256
NFX = 64
NFY = 512
N_GX = 8
N_GY = 4


def draw_neighbours(key, part):
    subtree_size = CL_DEV * N_GX
    span_size = 2 * CL_DEV
    scores = jax.random.randint(jax.random.fold_in(key, 11), (NC, span_size), 0, 1 << 20) * span_size + jnp.arange(span_size, dtype=jnp.int32)[None, :]
    picked = jnp.argsort(scores, axis=1, stable=True)[:, :NB - 1].astype(jnp.int32)
    shifted = jnp.where(picked < CL_DEV, picked - CL_DEV, picked - CL_DEV + 1)
    local_ids = (jnp.arange(NC, dtype=jnp.int32) % subtree_size)[:, None]
    others = (local_ids + shifted) % subtree_size
    return jnp.concatenate([local_ids, others], axis=1).astype(jnp.int32)


def draw_near_counts(key, part):
    devices = N_GX * N_GY
    heavy_device = jax.random.randint(jax.random.fold_in(key, 21), (devices,), 0, 8) == 0
    lighter = jax.random.randint(jax.random.fold_in(key, 22), (NC,), 1, 4)
    heavier = jnp.minimum(jax.random.randint(jax.random.fold_in(key, 23), (NC,), 5, NB + 4), NB)
    cluster_ids = jnp.arange(NC, dtype=jnp.int32)
    chosen = jnp.where(heavy_device[cluster_ids // CL_DEV], heavier, lighter)
    pinned = jax.random.randint(jax.random.fold_in(key, 24), (), 0, NC)
    return jnp.where(cluster_ids == pinned, NB, chosen).astype(jnp.int32)


def draw_cell_index(key, part):
    band_rows = FX_DEV * N_GX
    cluster_ids = jnp.arange(NC, dtype=jnp.int32)
    column = cluster_ids % (CL_DEV * N_GX) // CL_DEV
    offsets = jax.random.randint(jax.random.fold_in(key, 31), (NC, CSIZE), -FX_DEV, 2 * FX_DEV - 1)
    first_row = (column[:, None] * FX_DEV + offsets) % band_rows
    next_row = (first_row + 1) % band_rows
    first_col = jax.random.randint(jax.random.fold_in(key, 32), (NC, CSIZE), 0, FY_DEV - 1)
    rows = jnp.stack([first_row, next_row, first_row, next_row], axis=1)
    cols = jnp.stack([first_col, first_col, first_col + 1, first_col + 1], axis=1)
    return (rows * FY_DEV + cols).astype(jnp.int32)


def with_ends(entries, stream_key, least, top_value):
    longest = entries.shape.index(max(entries.shape))
    spots = []
    for shift in (0, 1):
        where = [jax.random.randint(jax.random.fold_in(stream_key, axis), (), 0, length) for axis, length in enumerate(entries.shape)]
        where[longest] = (where[longest] + shift) % entries.shape[longest]
        spots.append(tuple(where))
    return entries.at[spots[0]].set(least).at[spots[1]].set(top_value)


def shard_levels(stream_key, dims, pieces, low, top_value):
    factor_of = 1.0
    for axis_at, shards_of in pieces:
        steps = jax.random.uniform(jax.random.fold_in(jax.random.fold_in(stream_key, 6), axis_at), (shards_of,), jnp.float32, low / len(pieces), top_value / len(pieces))
        factor_of = factor_of * jnp.repeat(jnp.exp(steps), dims[axis_at] // shards_of).reshape((-1,) + (1,) * (len(dims) - 1 - axis_at))
    return factor_of


def gaussian(own_key, dims, width, reach, pieces=(), kind=jnp.bfloat16):
    array = width * jax.random.normal(own_key, dims, jnp.float32)
    if pieces:
        array = array * shard_levels(own_key, dims, pieces, -0.22, 0.18)
    return jnp.clip(array, -reach, reach).astype(kind)


def setup_inputs(seed: int = 0) -> dict:
    key_list = jax.random.split(jax.random.key(seed), 18)
    return {
        "slip_field": gaussian(key_list[0], (NC, 3, CSIZE), 1.0, 6.0, ((0, 32),), jnp.float32),
        "positions": gaussian(key_list[1], (NC, 3, CSIZE), 1.0, 6.0, ((0, 32),), jnp.float32),
        "neighbours": draw_neighbours(jax.random.fold_in(key_list[17], 71), 0),
        "near_counts": draw_near_counts(jax.random.fold_in(key_list[17], 71), 0),
        "cluster_basis": gaussian(key_list[4], (NC, RANK, 3, CSIZE), (24 * CL_DEV) ** -0.5, 0.4375, ((0, 32),), jnp.float32),
        "transfer": gaussian(key_list[5], (NODES, RANK, RANK), (2 * RANK) ** -0.5, 1.0, (), jnp.float32),
        "coupling": gaussian(key_list[6], (NODES, RANK, RANK), RANK ** -0.5, 1.5, (), jnp.float32),
        "prestress": gaussian(key_list[7], (NC, 3, CSIZE), 1.0, 6.0, ((0, 32),), jnp.float32),
        "normal_stress": jnp.clip(1.0 + 2.0 * jax.random.uniform(key_list[8], (NC, CSIZE), jnp.float32) ** shard_levels(key_list[8], (NC, CSIZE), ((0, 32),), -0.2, 0.2), 1.0, 3.0),
        "friction": jnp.clip(jnp.exp(math.log(0.9) - 1.0986122 * jax.random.uniform(key_list[9], (NC, CSIZE), jnp.float32) ** shard_levels(key_list[9], (NC, CSIZE), ((0, 32),), -0.2, 0.2)), 0.3, 0.9),
        "compliance": jnp.clip(jnp.exp(math.log(1.0) - 2.3025851 * jax.random.uniform(key_list[10], (NC, CSIZE), jnp.float32) ** shard_levels(key_list[10], (NC, CSIZE), ((0, 32),), -0.2, 0.2)), 0.1, 1.0),
        "slip_state": with_ends((jax.random.randint(key_list[11], (NC, CSIZE), 0, 2) < 1).astype(jnp.int32), jax.random.fold_in(key_list[11], 1), 0, 1),
        "cell_index": draw_cell_index(jax.random.fold_in(key_list[17], 71), 0),
        "cell_weight": jnp.clip(0.1 + 0.4 * jax.random.uniform(key_list[13], (NC, IW, CSIZE), jnp.float32) ** shard_levels(key_list[13], (NC, IW, CSIZE), ((0, 32),), -0.2, 0.2), 0.1, 0.5),
        "dilation": jnp.clip(jnp.exp(math.log(10.0) - 2.3025851 * jax.random.uniform(key_list[14], (NC, CSIZE), jnp.float32) ** shard_levels(key_list[14], (NC, CSIZE), ((0, 32),), -0.2, 0.2)), 1.0, 10.0),
        "pressure": gaussian(key_list[15], (NFX, NFY), 0.5, 4.0, ((0, 8), (1, 4)), jnp.float32),
        "mobility": jnp.clip(jnp.exp(math.log(0.24) - 1.5686159 * jax.random.uniform(key_list[16], (NFX, NFY), jnp.float32) ** shard_levels(key_list[16], (NFX, NFY), ((0, 8), (1, 4)), -0.2, 0.2)), 0.05, 0.24),
    }


HIGHEST = lax.Precision.HIGHEST
KERNEL_SCALE = 0.04
SOFTENING = 0.25

def pair_blocks(targets, sources, slipped):
    offsets = targets[:, :, :, None] - sources[:, :, None, :]
    radius = lax.optimization_barrier(jnp.sum(offsets * offsets, axis=1)) + SOFTENING
    inverse = lax.rsqrt(radius)
    inverse_cube = inverse * inverse * inverse
    projected = lax.optimization_barrier(jnp.sum(offsets * slipped[:, :, None, :], axis=1))
    direct = lax.optimization_barrier(jnp.sum(inverse[:, None] * slipped[:, :, None, :], axis=3))
    dyadic = lax.optimization_barrier(jnp.sum(offsets * (projected * inverse_cube)[:, None], axis=3))
    return KERNEL_SCALE * (direct + dyadic)

def reference(slip_field, positions, neighbours, near_counts, cluster_basis, transfer, coupling, prestress, normal_stress, friction, compliance, slip_state, cell_index, cell_weight, dilation, pressure, mobility):
    subtree_size = CL_DEV * N_GX
    devices = N_GX * N_GY
    levels = devices.bit_length() - 1
    cluster_ids = jnp.arange(NC, dtype=jnp.int32)
    source_ids = (cluster_ids // subtree_size * subtree_size)[:, None] + neighbours
    slot_ids = jnp.arange(NB, dtype=jnp.int32)
    active = slot_ids[None, :] < near_counts[:, None]
    band_size = NFX * FY_DEV
    global_cells = (cluster_ids // subtree_size)[:, None, None] * band_size + cell_index
    state_mask = slip_state.astype(jnp.float32)
    for outer_step in range(ITERS):

        def near_cluster(packed):
            own_id, source_row, active_row = packed
            targets = jnp.broadcast_to(positions[own_id], (NB, 3, CSIZE))
            blocks = pair_blocks(targets, positions[source_row], slip_field[source_row])
            return lax.optimization_barrier(jnp.sum(jnp.where(active_row[:, None, None], blocks, 0.0), axis=0))
        near_part = lax.map(near_cluster, (cluster_ids, source_ids, active))
        moments = jnp.einsum('ckia,cia->ck', cluster_basis, slip_field, precision=HIGHEST)
        moments = moments.reshape(devices, CL_DEV, RANK).sum(axis=1)
        tier_moments = [moments]
        for tier_level in range(levels):
            node_count = devices >> tier_level
            node_base = 2 * devices - 2 * node_count
            lifted = jnp.einsum('nmk,nm->nk', transfer[node_base:node_base + node_count], tier_moments[-1], precision=HIGHEST)
            tier_moments.append(lifted[0::2] + lifted[1::2])
        incoming = jnp.zeros((1, RANK), jnp.float32)
        for tier_level in reversed(range(levels)):
            node_count = devices >> tier_level
            node_base = 2 * devices - 2 * node_count
            node_ids = jnp.arange(node_count, dtype=jnp.int32)
            parent_field = incoming[node_ids // 2]
            sibling = tier_moments[tier_level][jnp.bitwise_xor(node_ids, 1)]
            incoming = jnp.einsum('nmk,nk->nm', transfer[node_base:node_base + node_count], parent_field, precision=HIGHEST) + jnp.einsum('nmk,nk->nm', coupling[node_base:node_base + node_count], sibling, precision=HIGHEST)
        far_part = jnp.einsum('ckia,ck->cia', cluster_basis, incoming[cluster_ids // CL_DEV], precision=HIGHEST)
        pressure_bands = pressure.reshape(NFX, N_GY, FY_DEV).transpose(1, 0, 2).reshape(-1)
        at_elements = lax.optimization_barrier(jnp.sum(cell_weight * pressure_bands[global_cells], axis=1))
        stress = prestress - (near_part + far_part)
        effective = normal_stress - at_elements
        magnitude = jnp.sqrt(lax.optimization_barrier(jnp.sum(stress * stress, axis=1)) + 1.0)
        factor = jnp.maximum(1.0 - friction * effective / magnitude, 0.0)
        step_slip = (state_mask * compliance * factor)[:, None, :] * stress
        slip_field = slip_field + step_slip
        dilated = dilation * lax.optimization_barrier(jnp.sum(step_slip * step_slip, axis=1))
        loaded = jax.ops.segment_sum((cell_weight * dilated[:, None, :]).reshape(-1), global_cells.reshape(-1), num_segments=N_GY * band_size)
        source = loaded.reshape(N_GY, NFX, FY_DEV).transpose(1, 0, 2).reshape(NFX, NFY)
        pressure = pressure + source
        for flow_step in range(FLOW_STEPS):
            padded = jnp.pad(pressure, 1)
            beside_all = padded[2:, 1:-1] + padded[:-2, 1:-1] + padded[1:-1, 2:] + padded[1:-1, :-2]
            pressure = pressure + mobility * (beside_all - 4.0 * pressure)
    return (slip_field, pressure)
```

```python
import functools

import jax
import jax.numpy as jnp
from jax import lax
from jax.experimental import pallas as pl
from jax.experimental.pallas import tpu as pltpu
from jax.sharding import PartitionSpec as P

ITERS = 2
FLOW_STEPS = 2
HIGHEST = lax.Precision.HIGHEST
KERNEL_SCALE = 0.04
SOFTENING = 0.25
MESH = pl.DeviceIdType.MESH
AROUND = ((-1, 0), (1, 0), (0, -1), (0, 1), (-1, -1), (-1, 1), (1, -1), (1, 1))
NT = (((1,), (1,)), ((), ()))


def kernel(
    nx, ny, levels,
    nbr_ref, count_ref, slip_ref, pos_ref, basis_ref, transfer_ref, coupling_ref,
    prestress_ref, normal_ref, friction_ref, compliance_ref, state_ref,
    cell_ref, weight_ref, dilation_ref, pressure_ref, mobility_ref,
    out_slip, out_pressure,
    path_t, path_c, pos_halo, slip_halo, slip_now, pos_b, slip_b, near_acc, far_s,
    moment_out, moment_in, row_w, col_hot, at_s, dil_s,
    p_now, p_halo, src_out, src_in, flow_in, mob_in,
    local_sem, send_sem, recv_sem, msend_sem, mrecv_sem,
):
    gx = lax.axis_index("gx")
    gy = lax.axis_index("gy")
    flat = gy * nx + gx
    devices = nx * ny
    comps, clusters, csize = slip_ref.shape
    slots = nbr_ref.shape[1]
    rank = basis_ref.shape[2]
    frows, fcols = pressure_ref.shape
    width = moment_out.shape[-1]
    subtree = clusters * nx
    strips = csize // 8

    barrier = pltpu.get_barrier_semaphore()

    def greet(step, carry):
        other = lax.rem(flat + step, devices)
        pl.semaphore_signal(
            barrier, inc=1,
            device_id={"gx": lax.rem(other, nx), "gy": lax.div(other, nx)},
            device_id_type=MESH,
        )
        return carry

    lax.fori_loop(1, devices, greet, 0)

    local = []
    for level in range(levels):
        node = 2 * devices - 2 * (devices >> level) + lax.div(flat, 1 << level)
        local.append(pltpu.make_async_copy(transfer_ref.at[node], path_t.at[level], local_sem.at[level]))
        local.append(pltpu.make_async_copy(coupling_ref.at[node], path_c.at[level], local_sem.at[levels + level]))
    for copy in local:
        copy.start()

    def remote(src, dst, number, dgx, dgy):
        return pltpu.make_async_remote_copy(
            src_ref=src, dst_ref=dst,
            send_sem=send_sem.at[number], recv_sem=recv_sem.at[number],
            device_id={"gx": lax.rem(gx + dgx + nx, nx), "gy": lax.rem(gy + dgy + ny, ny)},
            device_id_type=MESH,
        )

    started = []

    def send(src, dst, number, dgx, dgy):
        copy = remote(src, dst, number, dgx, dgy)
        copy.start()
        started.append(copy)
        return copy

    def send_both(src_back, src_ahead, dst, number):
        ahead = send(src_ahead, dst.at[0], number, 1, 0)
        back = send(src_back, dst.at[1], number + 1, -1, 0)
        return [ahead, back]

    def wait_in(copies):
        for copy in copies:
            copy.wait_recv()

    def spread(table, ref, base):
        def body(i, carry):
            columns = jnp.transpose(ref[i])
            for c in range(clusters):
                table[base + c, i] = jnp.broadcast_to(columns[:, c : c + 1], (csize, csize))
            return carry
        lax.fori_loop(0, comps, body, 0)

    def spread_own(table, ref):
        spread(table, ref, clusters)

    def spread_halo(table, ref):
        spread(table, ref.at[0], 0)
        spread(table, ref.at[1], 2 * clusters)

    def near(first, last):
        def one_cluster(c, carry):
            targets = [jnp.broadcast_to(pos_ref[i, pl.ds(c, 1), :], (8, csize)) for i in range(comps)]

            def one_slot(k, sums):
                number = nbr_ref[c, k]
                place = lax.rem(number - gx * clusters + clusters + subtree, subtree)
                place = jnp.minimum(place, 3 * clusters - 1)
                slipping = jnp.where(k < count_ref[c], place, 3 * clusters)
                sums = list(sums)
                for strip in range(strips):
                    rows = pl.ds(strip * 8, 8)
                    r = [targets[i] - pos_b[place, i, rows, :] for i in range(comps)]
                    s = [slip_b[slipping, i, rows, :] for i in range(comps)]
                    q = (r[0] * r[0] + r[1] * r[1]) + (r[2] * r[2] + SOFTENING)
                    inverse = lax.rsqrt(q)
                    along = (r[0] * s[0] + r[1] * s[1]) + r[2] * s[2]
                    scaled = along * (inverse * inverse)
                    for i in range(comps):
                        sums[i] = sums[i] + inverse * (s[i] + r[i] * scaled)
                return tuple(sums)

            if first == 0:
                start = tuple(jnp.zeros((8, csize), jnp.float32) for _ in range(comps))
            else:
                start = tuple(near_acc[i, c] for i in range(comps))
            sums = lax.fori_loop(first, last, one_slot, start)
            for i in range(comps):
                near_acc[i, c] = sums[i]
            return carry

        lax.fori_loop(0, clusters, one_cluster, 0)

    def moment_row(ref, lift):
        total = jnp.zeros((rank, csize), jnp.float32)
        for c in range(clusters):
            for i in range(comps):
                total = total + basis_ref[c, i] * ref[i, c : c + 1, :]
        column = jnp.sum(total, axis=1, keepdims=True)
        return jnp.sum(column * lift, axis=0, keepdims=True)

    def send_moments(it, ref, lift):
        moment_out[it] = moment_row(ref, lift)
        moment_in[it, flat] = jnp.zeros((1, width), jnp.float32)

        def body(step, carry):
            other = lax.rem(flat + step, devices)
            pltpu.make_async_remote_copy(
                src_ref=moment_out.at[it], dst_ref=moment_in.at[it, flat],
                send_sem=msend_sem.at[it], recv_sem=mrecv_sem.at[it],
                device_id={"gx": lax.rem(other, nx), "gy": lax.div(other, nx)},
                device_id_type=MESH,
            ).start()
            return carry

        lax.fori_loop(1, devices, body, 0)

    def wait_moments(it, sem):
        block = moment_in.at[it, pl.ds(0, devices - 1)]
        pltpu.make_async_copy(block, block, sem.at[it]).wait()

    spread_own(pos_b, pos_ref)
    spread_own(slip_b, slip_ref)
    slip_b[3 * clusters] = jnp.zeros((comps, csize, csize), jnp.float32)

    lane_rows = lax.broadcasted_iota(jnp.int32, (3 * frows, csize), 0)
    col_rows = lax.broadcasted_iota(jnp.int32, (fcols, csize), 0)
    first_cell = cell_ref[:, 0, :]
    cell_row = lax.div(first_cell, fcols)
    cell_col = first_cell - cell_row * fcols
    band_rows = frows * nx
    rim_row = lax.rem(cell_row - gx * frows + frows + band_rows, band_rows)
    for c in range(clusters):
        here = lane_rows == rim_row[c : c + 1, :]
        below = lane_rows == rim_row[c : c + 1, :] + 1
        w = [weight_ref[c, k : k + 1, :] for k in range(4)]
        row_w[c, 0] = jnp.where(here, w[0], 0.0) + jnp.where(below, w[1], 0.0)
        row_w[c, 1] = jnp.where(here, w[2], 0.0) + jnp.where(below, w[3], 0.0)
        hot = jnp.where(col_rows == cell_col[c : c + 1, :], 1.0, 0.0)
        col_hot[c] = hot.astype(jnp.bfloat16)

    for copy in local:
        copy.wait()
    place_rows = lax.broadcasted_iota(jnp.int32, (rank, width), 0)
    place_lanes = lax.broadcasted_iota(jnp.int32, (rank, width), 1)
    dot = functools.partial(jnp.dot, precision=HIGHEST, preferred_element_type=jnp.float32)
    chain = jnp.where(
        lax.broadcasted_iota(jnp.int32, (rank, rank), 0) == lax.broadcasted_iota(jnp.int32, (rank, rank), 1),
        1.0, 0.0,
    )
    lift = jnp.zeros((rank, width), jnp.float32)
    across = jnp.zeros((rank, width), jnp.float32)
    for level in range(levels):
        put = jnp.where(place_lanes == place_rows + level * rank, 1.0, 0.0)
        lift = lift + dot(chain, put)
        across = across + dot(dot(chain, path_c[level]), put)
        if level + 1 < levels:
            chain = dot(chain, path_t[level])

    node_ids = lax.broadcasted_iota(jnp.int32, (devices, width), 0)
    lane_level = lax.div(lax.broadcasted_iota(jnp.int32, (devices, width), 1), rank)
    sibling_mask = jnp.zeros((devices, width), jnp.bool_)
    for level in range(levels):
        own = lax.div(flat, 1 << level)
        sibling = own + 1 - 2 * lax.rem(own, 2)
        sibling_mask = sibling_mask | ((lane_level == level) & (lax.shift_right_logical(node_ids, level) == sibling))

    pl.semaphore_wait(barrier, devices - 1)

    base = 0
    waits_slip = send_both(slip_ref, slip_ref, slip_halo.at[0], base)
    waits_pos = send_both(pos_ref, pos_ref, pos_halo, base + 2)
    send_moments(0, slip_ref, lift)
    waits_p = send_both(pressure_ref, pressure_ref, p_halo.at[0], base + 4)
    waits_mob = []
    for number, (dgx, dgy) in enumerate(AROUND[:4]):
        waits_mob.append(send(mobility_ref, mob_in.at[number], base + 6 + number, -dgx, -dgy))
    base = base + 10

    near(0, 1)
    wait_in(waits_slip)
    wait_in(waits_pos)
    spread_halo(slip_b, slip_halo.at[0])
    spread_halo(pos_b, pos_halo)
    near(1, slots)
    wait_in(waits_mob)

    lanes = lax.broadcasted_iota(jnp.int32, (3 * frows, fcols), 1)
    inside = []
    for dgx, dgy in AROUND:
        ok = jnp.bool_(True)
        if dgx:
            ok = ok & (gx + dgx >= 0) & (gx + dgx < nx)
        if dgy:
            ok = ok & (gy + dgy >= 0) & (gy + dgy < ny)
        inside.append(jnp.where(ok, 1.0, 0.0))
    blank = jnp.zeros((frows, fcols), jnp.float32)
    mob_mid = jnp.concatenate([mob_in[0] * inside[0], mobility_ref[...], mob_in[1] * inside[1]], axis=0)
    mob_left = jnp.concatenate([blank, mob_in[2] * inside[2], blank], axis=0)
    mob_right = jnp.concatenate([blank, mob_in[3] * inside[3], blank], axis=0)
    rows3 = 3 * frows

    def stencil(mid, before, behind, mobility):
        beside = pltpu.roll(mid, 1, 0) + pltpu.roll(mid, rows3 - 1, 0)
        left = jnp.where(lanes == 0, pltpu.roll(before, 1, 1), pltpu.roll(mid, 1, 1))
        right = jnp.where(lanes == fcols - 1, pltpu.roll(behind, fcols - 1, 1), pltpu.roll(mid, fcols - 1, 1))
        return mid + mobility * ((beside + (left + right)) - 4.0 * mid)

    pressure = pressure_ref[...]
    old_slip = slip_ref
    for it in range(ITERS):
        last = it == ITERS - 1
        wait_moments(it, mrecv_sem)
        gathered = moment_in[it].reshape(devices, width)
        siblings = jnp.sum(jnp.where(sibling_mask, gathered, 0.0), axis=0, keepdims=True)
        incoming = jnp.sum(across * siblings, axis=1, keepdims=True)
        for c in range(clusters):
            for i in range(comps):
                far_s[i, c : c + 1, :] = jnp.sum(basis_ref[c, i] * incoming, axis=0, keepdims=True)
        wait_in(waits_p)
        table = jnp.concatenate([p_halo[it, 0], pressure, p_halo[it, 1]], axis=0)
        for c in range(clusters):
            columns = jnp.broadcast_to(cell_col[c : c + 1, :], (rows3, csize))
            g0 = jnp.take_along_axis(table, columns, axis=1)
            g1 = jnp.take_along_axis(pltpu.roll(table, fcols - 1, 1), columns, axis=1)
            at_s[c : c + 1, :] = jnp.sum(row_w[c, 0] * g0 + row_w[c, 1] * g1, axis=0, keepdims=True)
        stress = []
        for i in range(comps):
            near_part = KERNEL_SCALE * jnp.sum(near_acc[i], axis=1)
            stress.append(prestress_ref[i] - (near_part + far_s[i]))
        square = (stress[0] * stress[0] + stress[1] * stress[1]) + stress[2] * stress[2]
        effective = normal_ref[...] - at_s[...]
        factor = jnp.maximum(1.0 - friction_ref[...] * effective / jnp.sqrt(square + 1.0), 0.0)
        scale = state_ref[...].astype(jnp.float32) * compliance_ref[...] * factor
        step = [scale * stress[i] for i in range(comps)]
        target = out_slip if last else slip_now
        for i in range(comps):
            target[i] = old_slip[i] + step[i]
        old_slip = target
        if not last:
            waits_slip = send_both(slip_now, slip_now, slip_halo.at[it + 1], base)
            base = base + 2
            send_moments(it + 1, slip_now, lift)
        dil_s[...] = dilation_ref[...] * ((step[0] * step[0] + step[1] * step[1]) + step[2] * step[2])
        loaded = jnp.zeros((4 * rows3, fcols), jnp.float32)
        for c in range(clusters):
            dilated = dil_s[c : c + 1, :]
            left = jnp.concatenate([row_w[c, 0] * dilated, row_w[c, 1] * dilated], axis=0)
            high = left.astype(jnp.bfloat16)
            low = (left - high.astype(jnp.float32)).astype(jnp.bfloat16)
            loaded = loaded + lax.dot_general(
                jnp.concatenate([high, low], axis=0), col_hot[c], NT,
                preferred_element_type=jnp.float32,
            )
        loaded = loaded[: 2 * rows3] + loaded[2 * rows3 :]
        loaded = loaded[:rows3] + pltpu.roll(loaded[rows3:], 1, 1)
        src_out[it, 0] = loaded[:frows]
        src_out[it, 1] = loaded[2 * frows :]
        waits_src = send_both(src_out.at[it, 0], src_out.at[it, 1], src_in.at[it], base)
        base = base + 2
        if not last:
            spread_own(slip_b, slip_now)
            near(0, 1)
        wait_in(waits_src)
        pressure = pressure + (loaded[frows : 2 * frows] + (src_in[it, 0] + src_in[it, 1]))
        p_now[2 * it] = pressure
        waits_flow = []
        for number, (dgx, dgy) in enumerate(AROUND):
            waits_flow.append(send(p_now.at[2 * it], flow_in.at[it, number], base, -dgx, -dgy))
            base = base + 1
        if not last:
            wait_in(waits_slip)
            spread_halo(slip_b, slip_halo.at[it + 1])
            near(1, slots // 2)
        wait_in(waits_flow)
        around = [flow_in[it, number] * inside[number] for number in range(8)]
        mid = jnp.concatenate([around[0], pressure, around[1]], axis=0)
        before = jnp.concatenate([around[4], around[2], around[6]], axis=0)
        behind = jnp.concatenate([around[5], around[3], around[7]], axis=0)
        mid1 = stencil(mid, before, behind, mob_mid)
        before1 = stencil(before, before, mid, mob_left)
        behind1 = stencil(behind, mid, behind, mob_right)
        pressure = stencil(mid1, before1, behind1, mob_mid)[frows : 2 * frows]
        if last:
            out_pressure[...] = pressure
        else:
            p_now[2 * it + 1] = pressure
            waits_p = send_both(p_now.at[2 * it + 1], p_now.at[2 * it + 1], p_halo.at[it + 1], base)
            base = base + 2
            near(slots // 2, slots)

    for copy in started:
        copy.wait_send()
    for it in range(ITERS):
        wait_moments(it, msend_sem)


def shards(
    slip_field, positions, neighbours, near_counts, cluster_basis, transfer, coupling,
    prestress, normal_stress, friction, compliance, slip_state, cell_index, cell_weight,
    dilation, pressure, mobility,
):
    nx = lax.axis_size("gx")
    ny = lax.axis_size("gy")
    devices = nx * ny
    levels = devices.bit_length() - 1
    slip_field, positions, prestress = (
        jnp.transpose(x, (1, 0, 2)) for x in (slip_field, positions, prestress)
    )
    cluster_basis = jnp.transpose(cluster_basis, (0, 2, 1, 3))
    comps, clusters, csize = slip_field.shape
    rank = transfer.shape[1]
    frows, fcols = pressure.shape
    width = (levels * rank + 127) // 128 * 128
    f32 = jnp.float32
    copies = 10 + ITERS * 14
    vmem = pl.BlockSpec(memory_space=pltpu.VMEM)
    smem = pl.BlockSpec(memory_space=pltpu.SMEM)
    hbm = pl.BlockSpec(memory_space=pl.ANY)
    new_slip, new_pressure = pl.pallas_call(
        functools.partial(kernel, nx, ny, levels),
        out_shape=(
            jax.ShapeDtypeStruct(slip_field.shape, f32),
            jax.ShapeDtypeStruct(pressure.shape, f32),
        ),
        in_specs=[smem, smem, vmem, vmem, vmem, hbm, hbm] + [vmem] * 10,
        out_specs=(vmem, vmem),
        scratch_shapes=[
            pltpu.VMEM((levels, rank, rank), f32),
            pltpu.VMEM((levels, rank, rank), f32),
            pltpu.VMEM((2,) + slip_field.shape, f32),
            pltpu.VMEM((ITERS, 2) + slip_field.shape, f32),
            pltpu.VMEM(slip_field.shape, f32),
            pltpu.VMEM((3 * clusters, comps, csize, csize), f32),
            pltpu.VMEM((3 * clusters + 1, comps, csize, csize), f32),
            pltpu.VMEM((comps, clusters, 8, csize), f32),
            pltpu.VMEM(slip_field.shape, f32),
            pltpu.VMEM((ITERS, 1, width), f32),
            pltpu.VMEM((ITERS, devices, 1, width), f32),
            pltpu.VMEM((clusters, 2, 3 * frows, csize), f32),
            pltpu.VMEM((clusters, fcols, csize), jnp.bfloat16),
            pltpu.VMEM((clusters, csize), f32),
            pltpu.VMEM((clusters, csize), f32),
            pltpu.VMEM((2 * ITERS, frows, fcols), f32),
            pltpu.VMEM((ITERS, 2, frows, fcols), f32),
            pltpu.VMEM((ITERS, 2, frows, fcols), f32),
            pltpu.VMEM((ITERS, 2, frows, fcols), f32),
            pltpu.VMEM((ITERS, 8, frows, fcols), f32),
            pltpu.VMEM((4, frows, fcols), f32),
            pltpu.SemaphoreType.DMA((2 * levels,)),
            pltpu.SemaphoreType.DMA((copies,)),
            pltpu.SemaphoreType.DMA((copies,)),
            pltpu.SemaphoreType.DMA((ITERS,)),
            pltpu.SemaphoreType.DMA((ITERS,)),
        ],
        compiler_params=pltpu.CompilerParams(collective_id=0, has_side_effects=True),
        name="coupling",
    )(
        neighbours, near_counts, slip_field, positions, cluster_basis, transfer, coupling,
        prestress, normal_stress, friction, compliance, slip_state,
        cell_index, cell_weight, dilation, pressure, mobility,
    )
    return jnp.transpose(new_slip, (1, 0, 2)), new_pressure


def solution(mesh):
    by_cluster = ("gy", "gx")
    in_specs = (
        P(by_cluster, None, None),
        P(by_cluster, None, None),
        P(by_cluster, None),
        P(by_cluster),
        P(by_cluster, None, None, None),
        P(),
        P(),
        P(by_cluster, None, None),
        P(by_cluster, None),
        P(by_cluster, None),
        P(by_cluster, None),
        P(by_cluster, None),
        P(by_cluster, None, None),
        P(by_cluster, None, None),
        P(by_cluster, None),
        P("gx", "gy"),
        P("gx", "gy"),
    )
    out_specs = (P(by_cluster, None, None), P("gx", "gy"))
    return jax.shard_map(shards, mesh=mesh, in_specs=in_specs, out_specs=out_specs, check_vma=False)
```

```python
import functools

import jax
import jax.numpy as jnp
from jax import lax
from jax.experimental import pallas as pl
from jax.experimental.pallas import tpu as pltpu
from jax.sharding import PartitionSpec as P

ITERS = 2
FLOW_STEPS = 2
HIGHEST = lax.Precision.HIGHEST
KERNEL_SCALE = 0.04
SOFTENING = 0.25
MESH = pl.DeviceIdType.MESH
AROUND = ((-1, 0), (1, 0), (0, -1), (0, 1), (-1, -1), (-1, 1), (1, -1), (1, 1))
NT = (((1,), (1,)), ((), ()))


def kernel(
    nx, ny, levels,
    nbr_ref, count_ref, slip_ref, pos_ref, basis_ref, transfer_ref, coupling_ref,
    prestress_ref, normal_ref, friction_ref, compliance_ref, state_ref,
    cell_ref, weight_ref, dilation_ref, pressure_ref, mobility_ref,
    out_slip, out_pressure,
    pos_halo, slip_halo, slip_now, pos_b, slip_b, near_acc, far_s,
    moment_out, moment_in, row_w, col_hot, at_s, dil_s,
    p_now, p_halo, src_out, src_in, flow_in, mob_in,
    send_sem, recv_sem, msend_sem, mrecv_sem,
):
    gx = lax.axis_index("gx")
    gy = lax.axis_index("gy")
    flat = gy * nx + gx
    devices = nx * ny
    comps, clusters, csize = slip_ref.shape
    slots = nbr_ref.shape[1]
    rank = basis_ref.shape[2]
    frows, fcols = pressure_ref.shape
    width = moment_out.shape[-1]
    subtree = clusters * nx
    strips = csize // 8

    barrier = pltpu.get_barrier_semaphore()

    def greet(step, carry):
        other = lax.rem(flat + step, devices)
        pl.semaphore_signal(
            barrier, inc=1,
            device_id={"gx": lax.rem(other, nx), "gy": lax.div(other, nx)},
            device_id_type=MESH,
        )
        return carry

    lax.fori_loop(1, devices, greet, 0)

    def remote(src, dst, number, dgx, dgy):
        return pltpu.make_async_remote_copy(
            src_ref=src, dst_ref=dst,
            send_sem=send_sem.at[number], recv_sem=recv_sem.at[number],
            device_id={"gx": lax.rem(gx + dgx + nx, nx), "gy": lax.rem(gy + dgy + ny, ny)},
            device_id_type=MESH,
        )

    started = []

    def send(src, dst, number, dgx, dgy):
        copy = remote(src, dst, number, dgx, dgy)
        copy.start()
        started.append(copy)
        return copy

    def send_both(src_back, src_ahead, dst, number):
        ahead = send(src_ahead, dst.at[0], number, 1, 0)
        back = send(src_back, dst.at[1], number + 1, -1, 0)
        return [ahead, back]

    def wait_in(copies):
        for copy in copies:
            copy.wait_recv()

    def spread(table, ref, base):
        def body(i, carry):
            columns = jnp.transpose(ref[i])
            for c in range(clusters):
                table[base + c, i] = jnp.broadcast_to(columns[:, c : c + 1], (csize, csize))
            return carry
        lax.fori_loop(0, comps, body, 0)

    def spread_own(table, ref):
        spread(table, ref, clusters)

    def spread_halo(table, ref):
        spread(table, ref.at[0], 0)
        spread(table, ref.at[1], 2 * clusters)

    def near(first, last):
        def one_cluster(c, carry):
            targets = [jnp.broadcast_to(pos_ref[i, pl.ds(c, 1), :], (8, csize)) for i in range(comps)]

            def one_slot(k, sums):
                number = nbr_ref[c, k]
                place = lax.rem(number - gx * clusters + clusters + subtree, subtree)
                place = jnp.minimum(place, 3 * clusters - 1)
                slipping = jnp.where(k < count_ref[c], place, 3 * clusters)
                sums = list(sums)
                for strip in range(strips):
                    rows = pl.ds(strip * 8, 8)
                    r = [targets[i] - pos_b[place, i, rows, :] for i in range(comps)]
                    s = [slip_b[slipping, i, rows, :] for i in range(comps)]
                    q = (r[0] * r[0] + r[1] * r[1]) + (r[2] * r[2] + SOFTENING)
                    inverse = lax.rsqrt(q)
                    along = (r[0] * s[0] + r[1] * s[1]) + r[2] * s[2]
                    scaled = along * (inverse * inverse)
                    for i in range(comps):
                        sums[i] = sums[i] + inverse * (s[i] + r[i] * scaled)
                return tuple(sums)

            if first == 0:
                start = tuple(jnp.zeros((8, csize), jnp.float32) for _ in range(comps))
            else:
                start = tuple(near_acc[i, c] for i in range(comps))
            sums = lax.fori_loop(first, last, one_slot, start)
            for i in range(comps):
                near_acc[i, c] = sums[i]
            return carry

        lax.fori_loop(0, clusters, one_cluster, 0)

    def moment_row(ref, lift):
        total = jnp.zeros((rank, csize), jnp.float32)
        for c in range(clusters):
            for i in range(comps):
                total = total + basis_ref[c, i] * ref[i, c : c + 1, :]
        column = jnp.sum(total, axis=1, keepdims=True)
        return jnp.sum(column * lift, axis=0, keepdims=True)

    def send_moments(it, ref, lift):
        moment_out[it] = moment_row(ref, lift)
        moment_in[it, flat] = jnp.zeros((1, width), jnp.float32)

        def body(step, carry):
            other = lax.rem(flat + step, devices)
            pltpu.make_async_remote_copy(
                src_ref=moment_out.at[it], dst_ref=moment_in.at[it, flat],
                send_sem=msend_sem.at[it], recv_sem=mrecv_sem.at[it],
                device_id={"gx": lax.rem(other, nx), "gy": lax.div(other, nx)},
                device_id_type=MESH,
            ).start()
            return carry

        lax.fori_loop(1, devices, body, 0)

    def wait_moments(it, sem):
        block = moment_in.at[it, pl.ds(0, devices - 1)]
        pltpu.make_async_copy(block, block, sem.at[it]).wait()

    spread_own(pos_b, pos_ref)
    spread_own(slip_b, slip_ref)
    slip_b[3 * clusters] = jnp.zeros((comps, csize, csize), jnp.float32)

    lane_rows = lax.broadcasted_iota(jnp.int32, (3 * frows, csize), 0)
    col_rows = lax.broadcasted_iota(jnp.int32, (fcols, csize), 0)
    first_cell = cell_ref[:, 0, :]
    cell_row = lax.div(first_cell, fcols)
    cell_col = first_cell - cell_row * fcols
    band_rows = frows * nx
    rim_row = lax.rem(cell_row - gx * frows + frows + band_rows, band_rows)
    for c in range(clusters):
        here = lane_rows == rim_row[c : c + 1, :]
        below = lane_rows == rim_row[c : c + 1, :] + 1
        w = [weight_ref[c, k : k + 1, :] for k in range(4)]
        row_w[c, 0] = jnp.where(here, w[0], 0.0) + jnp.where(below, w[1], 0.0)
        row_w[c, 1] = jnp.where(here, w[2], 0.0) + jnp.where(below, w[3], 0.0)
        hot = jnp.where(col_rows == cell_col[c : c + 1, :], 1.0, 0.0)
        col_hot[c] = hot.astype(jnp.bfloat16)

    place_rows = lax.broadcasted_iota(jnp.int32, (rank, width), 0)
    place_lanes = lax.broadcasted_iota(jnp.int32, (rank, width), 1)
    dot = functools.partial(jnp.dot, precision=HIGHEST, preferred_element_type=jnp.float32)
    level_rows = (levels + 7) // 8 * 8
    nodes = transfer_ref.shape[2]
    row_level = lax.broadcasted_iota(jnp.int32, (level_rows, nodes), 0)
    node_lane = lax.broadcasted_iota(jnp.int32, (level_rows, nodes), 1)
    pick = jnp.zeros((level_rows, nodes), jnp.float32)
    for level in range(levels):
        node = 2 * devices - 2 * (devices >> level) + lax.div(flat, 1 << level)
        pick = pick + jnp.where((row_level == level) & (node_lane == node), 1.0, 0.0)
    square_lanes = lax.broadcasted_iota(jnp.int32, (rank, rank * rank), 1)
    square_rows = lax.broadcasted_iota(jnp.int32, (rank, rank * rank), 0)
    keep = lax.div(square_lanes, rank) == square_rows
    fold = jnp.where(
        lax.rem(lax.broadcasted_iota(jnp.int32, (rank * rank, rank), 0), rank)
        == lax.broadcasted_iota(jnp.int32, (rank * rank, rank), 1),
        1.0, 0.0,
    )

    def path_of(ref):
        flat_rows = lax.dot_general(
            pick, ref[...].reshape(rank * rank, nodes), NT,
            precision=HIGHEST, preferred_element_type=jnp.float32,
        )
        spread_rows = jnp.concatenate(
            [jnp.where(keep, flat_rows[level : level + 1], 0.0) for level in range(levels)], axis=0
        )
        folded = dot(spread_rows, fold)
        return [folded[level * rank : (level + 1) * rank] for level in range(levels)]

    path_t = path_of(transfer_ref)
    path_c = path_of(coupling_ref)
    chain = jnp.where(
        lax.broadcasted_iota(jnp.int32, (rank, rank), 0) == lax.broadcasted_iota(jnp.int32, (rank, rank), 1),
        1.0, 0.0,
    )
    lift = jnp.zeros((rank, width), jnp.float32)
    across = jnp.zeros((rank, width), jnp.float32)
    for level in range(levels):
        put = jnp.where(place_lanes == place_rows + level * rank, 1.0, 0.0)
        lift = lift + dot(chain, put)
        across = across + dot(dot(chain, path_c[level]), put)
        if level + 1 < levels:
            chain = dot(chain, path_t[level])

    node_ids = lax.broadcasted_iota(jnp.int32, (devices, width), 0)
    lane_level = lax.div(lax.broadcasted_iota(jnp.int32, (devices, width), 1), rank)
    sibling_mask = jnp.zeros((devices, width), jnp.bool_)
    for level in range(levels):
        own = lax.div(flat, 1 << level)
        sibling = own + 1 - 2 * lax.rem(own, 2)
        sibling_mask = sibling_mask | ((lane_level == level) & (lax.shift_right_logical(node_ids, level) == sibling))

    pl.semaphore_wait(barrier, devices - 1)

    base = 0
    waits_slip = send_both(slip_ref, slip_ref, slip_halo.at[0], base)
    waits_pos = send_both(pos_ref, pos_ref, pos_halo, base + 2)
    send_moments(0, slip_ref, lift)
    waits_p = send_both(pressure_ref, pressure_ref, p_halo.at[0], base + 4)
    waits_mob = []
    for number, (dgx, dgy) in enumerate(AROUND[:4]):
        waits_mob.append(send(mobility_ref, mob_in.at[number], base + 6 + number, -dgx, -dgy))
    base = base + 10

    near(0, 1)
    wait_in(waits_slip)
    wait_in(waits_pos)
    spread_halo(slip_b, slip_halo.at[0])
    spread_halo(pos_b, pos_halo)
    near(1, slots)
    wait_in(waits_mob)

    lanes = lax.broadcasted_iota(jnp.int32, (3 * frows, fcols), 1)
    inside = []
    for dgx, dgy in AROUND:
        ok = jnp.bool_(True)
        if dgx:
            ok = ok & (gx + dgx >= 0) & (gx + dgx < nx)
        if dgy:
            ok = ok & (gy + dgy >= 0) & (gy + dgy < ny)
        inside.append(jnp.where(ok, 1.0, 0.0))
    blank = jnp.zeros((frows, fcols), jnp.float32)
    mob_mid = jnp.concatenate([mob_in[0] * inside[0], mobility_ref[...], mob_in[1] * inside[1]], axis=0)
    mob_left = jnp.concatenate([blank, mob_in[2] * inside[2], blank], axis=0)
    mob_right = jnp.concatenate([blank, mob_in[3] * inside[3], blank], axis=0)
    rows3 = 3 * frows

    def stencil(mid, before, behind, mobility):
        beside = pltpu.roll(mid, 1, 0) + pltpu.roll(mid, rows3 - 1, 0)
        left = jnp.where(lanes == 0, pltpu.roll(before, 1, 1), pltpu.roll(mid, 1, 1))
        right = jnp.where(lanes == fcols - 1, pltpu.roll(behind, fcols - 1, 1), pltpu.roll(mid, fcols - 1, 1))
        return mid + mobility * ((beside + (left + right)) - 4.0 * mid)

    pressure = pressure_ref[...]
    old_slip = slip_ref
    for it in range(ITERS):
        last = it == ITERS - 1
        wait_moments(it, mrecv_sem)
        gathered = moment_in[it].reshape(devices, width)
        siblings = jnp.sum(jnp.where(sibling_mask, gathered, 0.0), axis=0, keepdims=True)
        incoming = jnp.sum(across * siblings, axis=1, keepdims=True)
        for c in range(clusters):
            for i in range(comps):
                far_s[i, c : c + 1, :] = jnp.sum(basis_ref[c, i] * incoming, axis=0, keepdims=True)
        wait_in(waits_p)
        table = jnp.concatenate([p_halo[it, 0], pressure, p_halo[it, 1]], axis=0)
        for c in range(clusters):
            columns = jnp.broadcast_to(cell_col[c : c + 1, :], (rows3, csize))
            g0 = jnp.take_along_axis(table, columns, axis=1)
            g1 = jnp.take_along_axis(pltpu.roll(table, fcols - 1, 1), columns, axis=1)
            at_s[c : c + 1, :] = jnp.sum(row_w[c, 0] * g0 + row_w[c, 1] * g1, axis=0, keepdims=True)
        stress = []
        for i in range(comps):
            near_part = KERNEL_SCALE * jnp.sum(near_acc[i], axis=1)
            stress.append(prestress_ref[i] - (near_part + far_s[i]))
        square = (stress[0] * stress[0] + stress[1] * stress[1]) + stress[2] * stress[2]
        effective = normal_ref[...] - at_s[...]
        factor = jnp.maximum(1.0 - friction_ref[...] * effective / jnp.sqrt(square + 1.0), 0.0)
        scale = state_ref[...].astype(jnp.float32) * compliance_ref[...] * factor
        step = [scale * stress[i] for i in range(comps)]
        target = out_slip if last else slip_now
        for i in range(comps):
            target[i] = old_slip[i] + step[i]
        old_slip = target
        if not last:
            waits_slip = send_both(slip_now, slip_now, slip_halo.at[it + 1], base)
            base = base + 2
            send_moments(it + 1, slip_now, lift)
        dil_s[...] = dilation_ref[...] * ((step[0] * step[0] + step[1] * step[1]) + step[2] * step[2])
        loaded = jnp.zeros((4 * rows3, fcols), jnp.float32)
        for c in range(clusters):
            dilated = dil_s[c : c + 1, :]
            left = jnp.concatenate([row_w[c, 0] * dilated, row_w[c, 1] * dilated], axis=0)
            high = left.astype(jnp.bfloat16)
            low = (left - high.astype(jnp.float32)).astype(jnp.bfloat16)
            loaded = loaded + lax.dot_general(
                jnp.concatenate([high, low], axis=0), col_hot[c], NT,
                preferred_element_type=jnp.float32,
            )
        loaded = loaded[: 2 * rows3] + loaded[2 * rows3 :]
        loaded = loaded[:rows3] + pltpu.roll(loaded[rows3:], 1, 1)
        src_out[it, 0] = loaded[:frows]
        src_out[it, 1] = loaded[2 * frows :]
        waits_src = send_both(src_out.at[it, 0], src_out.at[it, 1], src_in.at[it], base)
        base = base + 2
        if not last:
            spread_own(slip_b, slip_now)
            near(0, 1)
        wait_in(waits_src)
        pressure = pressure + (loaded[frows : 2 * frows] + (src_in[it, 0] + src_in[it, 1]))
        p_now[2 * it] = pressure
        waits_flow = []
        for number, (dgx, dgy) in enumerate(AROUND):
            waits_flow.append(send(p_now.at[2 * it], flow_in.at[it, number], base, -dgx, -dgy))
            base = base + 1
        if not last:
            wait_in(waits_slip)
            spread_halo(slip_b, slip_halo.at[it + 1])
            near(1, slots // 2)
        wait_in(waits_flow)
        around = [flow_in[it, number] * inside[number] for number in range(8)]
        mid = jnp.concatenate([around[0], pressure, around[1]], axis=0)
        before = jnp.concatenate([around[4], around[2], around[6]], axis=0)
        behind = jnp.concatenate([around[5], around[3], around[7]], axis=0)
        mid1 = stencil(mid, before, behind, mob_mid)
        before1 = stencil(before, before, mid, mob_left)
        behind1 = stencil(behind, mid, behind, mob_right)
        pressure = stencil(mid1, before1, behind1, mob_mid)[frows : 2 * frows]
        if last:
            out_pressure[...] = pressure
        else:
            p_now[2 * it + 1] = pressure
            waits_p = send_both(p_now.at[2 * it + 1], p_now.at[2 * it + 1], p_halo.at[it + 1], base)
            base = base + 2
            near(slots // 2, slots)

    for copy in started:
        copy.wait_send()
    for it in range(ITERS):
        wait_moments(it, msend_sem)


def shards(
    slip_field, positions, neighbours, near_counts, cluster_basis, transfer, coupling,
    prestress, normal_stress, friction, compliance, slip_state, cell_index, cell_weight,
    dilation, pressure, mobility,
):
    nx = lax.axis_size("gx")
    ny = lax.axis_size("gy")
    devices = nx * ny
    levels = devices.bit_length() - 1
    slip_field, positions, prestress = (
        jnp.transpose(x, (1, 0, 2)) for x in (slip_field, positions, prestress)
    )
    cluster_basis = jnp.transpose(cluster_basis, (0, 2, 1, 3))
    comps, clusters, csize = slip_field.shape
    rank = transfer.shape[1]
    transfer, coupling = (jnp.transpose(x, (1, 2, 0)) for x in (transfer, coupling))
    frows, fcols = pressure.shape
    width = (levels * rank + 127) // 128 * 128
    f32 = jnp.float32
    copies = 10 + ITERS * 14
    vmem = pl.BlockSpec(memory_space=pltpu.VMEM)
    smem = pl.BlockSpec(memory_space=pltpu.SMEM)
    new_slip, new_pressure = pl.pallas_call(
        functools.partial(kernel, nx, ny, levels),
        out_shape=(
            jax.ShapeDtypeStruct(slip_field.shape, f32),
            jax.ShapeDtypeStruct(pressure.shape, f32),
        ),
        in_specs=[smem, smem] + [vmem] * 15,
        out_specs=(vmem, vmem),
        scratch_shapes=[
            pltpu.VMEM((2,) + slip_field.shape, f32),
            pltpu.VMEM((ITERS, 2) + slip_field.shape, f32),
            pltpu.VMEM(slip_field.shape, f32),
            pltpu.VMEM((3 * clusters, comps, csize, csize), f32),
            pltpu.VMEM((3 * clusters + 1, comps, csize, csize), f32),
            pltpu.VMEM((comps, clusters, 8, csize), f32),
            pltpu.VMEM(slip_field.shape, f32),
            pltpu.VMEM((ITERS, 1, width), f32),
            pltpu.VMEM((ITERS, devices, 1, width), f32),
            pltpu.VMEM((clusters, 2, 3 * frows, csize), f32),
            pltpu.VMEM((clusters, fcols, csize), jnp.bfloat16),
            pltpu.VMEM((clusters, csize), f32),
            pltpu.VMEM((clusters, csize), f32),
            pltpu.VMEM((2 * ITERS, frows, fcols), f32),
            pltpu.VMEM((ITERS, 2, frows, fcols), f32),
            pltpu.VMEM((ITERS, 2, frows, fcols), f32),
            pltpu.VMEM((ITERS, 2, frows, fcols), f32),
            pltpu.VMEM((ITERS, 8, frows, fcols), f32),
            pltpu.VMEM((4, frows, fcols), f32),
            pltpu.SemaphoreType.DMA((copies,)),
            pltpu.SemaphoreType.DMA((copies,)),
            pltpu.SemaphoreType.DMA((ITERS,)),
            pltpu.SemaphoreType.DMA((ITERS,)),
        ],
        compiler_params=pltpu.CompilerParams(collective_id=0, has_side_effects=True),
        name="coupling",
    )(
        neighbours, near_counts, slip_field, positions, cluster_basis, transfer, coupling,
        prestress, normal_stress, friction, compliance, slip_state,
        cell_index, cell_weight, dilation, pressure, mobility,
    )
    return jnp.transpose(new_slip, (1, 0, 2)), new_pressure


def solution(mesh):
    by_cluster = ("gy", "gx")
    in_specs = (
        P(by_cluster, None, None),
        P(by_cluster, None, None),
        P(by_cluster, None),
        P(by_cluster),
        P(by_cluster, None, None, None),
        P(),
        P(),
        P(by_cluster, None, None),
        P(by_cluster, None),
        P(by_cluster, None),
        P(by_cluster, None),
        P(by_cluster, None),
        P(by_cluster, None, None),
        P(by_cluster, None, None),
        P(by_cluster, None),
        P("gx", "gy"),
        P("gx", "gy"),
    )
    out_specs = (P(by_cluster, None, None), P("gx", "gy"))
    return jax.shard_map(shards, mesh=mesh, in_specs=in_specs, out_specs=out_specs, check_vma=False)
```
